32 devices in a mesh: wide: 8 (over z, x), narrow: 4 (over y, core).
Axes of the slice: x: 2, y: 2, z: 4, core: 2. Of those that a mesh axis runs over, the one named last changes fastest.
Arguments:
- tokens: bfloat16 [16384, 2048], P(('wide', 'narrow')), may hold values from -6 to 6
- lengths: int32 [32], P(('wide', 'narrow')), may hold values from 1 to 512, 12288 in all
- in_weight: bfloat16 [2048, 8512], P(('wide', 'narrow')), may hold values from -0.125 to 0.125
- out_weight: bfloat16 [4096, 2048], P(('wide', 'narrow')), may hold values from -0.09375 to 0.09375
- norm_gain: bfloat16 [2048], P(('wide', 'narrow')), may hold values from 0.5 to 1.5
- conv_weight: bfloat16 [4352, 4], P(('wide', 'narrow')), may hold values from -3 to 3
- conv_bias: bfloat16 [4352], P(('wide', 'narrow')), may hold values from -0.5 to 0.5
- out_gain: bfloat16 [4096], P(('wide', 'narrow')), may hold values from 0.5 to 1.5
- a_log: float32 [64], P('wide'), may hold values from -3 to 1.6
- dt_bias: float32 [64], P('wide'), may hold values from -6 to -3
- d_skip: float32 [64], P('wide'), may hold values from 0.5 to 1.5
- cotangent: bfloat16 [16384, 2048], P(('wide', 'narrow')), may hold values from -6 to 6
Outputs:
- output: bfloat16 [16384, 2048], P(('wide', 'narrow'))
- token_grad: bfloat16 [16384, 2048], P(('wide', 'narrow'))
- in_weight_grad: float32 [2048, 8512], P(('wide', 'narrow'))
- out_weight_grad: float32 [4096, 2048], P(('wide', 'narrow'))
- norm_gain_grad: float32 [2048], P(('wide', 'narrow'))
- conv_weight_grad: float32 [4352, 4], P(('wide', 'narrow'))
- conv_bias_grad: float32 [4352], P(('wide', 'narrow'))
- out_gain_grad: float32 [4096], P(('wide', 'narrow'))
- a_log_grad: float32 [64], P('wide')
- dt_bias_grad: float32 [64], P('wide')
- d_skip_grad: float32 [64], P('wide')
The draws below stay inside these ranges and needn't reach their ends.
Inputs may be any that keep to these rules, and one draw needn't show every extreme that they name: `lengths`: each sequence's live tokens are the first rows of its 512 slots; the longest fills all of them.
All inputs are finite; a program needn't handle non-finite values. No bound on the sum of `lengths` on one device may be relied on, other than what follows from the above.
Results may differ from the reference program's by a relative error of at most 0.014.
Values may be sent and summed in bfloat16 or wider, within the bound.
No kernel may reach another device: no remote copies, remote signals or barrier semaphores. Data moves between devices by JAX's collectives and lax.ppermute only.
A program may use at most 448 MiB of HBM per device.

```python
import math
from functools import partial
import jax
import jax.numpy as jnp
import numpy as np
from jax import lax

D = 2048
HEADS = 64
HEAD_DIM = 64
NSTATE = 128
KCONV = 4
SPAN = 256
TOK_DEV = 512
DIN = 4096
CONV_CH = 4352
DPROJ = 8512
SEQS = 32
TOKENS = 16384


def level_of(rng, shape, split, low, top_value):
    factor_of, own = 1.0, jax.random.fold_in(rng, 6)
    for position, parts in split:
        steps = jnp.exp(jax.random.uniform(jax.random.fold_in(own, position), (parts,), jnp.float32, low / len(split), top_value / len(split)))
        factor_of = factor_of * jnp.repeat(steps, shape[position] // parts).reshape([-1 if axis == position else 1 for axis in range(len(shape))])
    return factor_of


def profile(amount, total, reach, lean):
    loads = [(1 << 20) // math.isqrt(grade ** lean) + 1 for grade in range(2, amount + 1)]
    spare, given = total - reach - (amount - 1), [1] * (amount - 1)
    while spare > 0:
        candidates = [i for i in range(amount - 1) if given[i] < reach]
        pool, left = sum([loads[i] for i in candidates]), spare
        for i in candidates:
            more = min(reach - given[i], max(1, left * loads[i] // pool), spare)
            given[i] = given[i] + more
            spare = spare - more
    return np.array([reach] + given)


def ragged_sizes(stream_key, amount, total, bound, lean):
    if amount == 2:
        one = jax.random.randint(stream_key, (), max(1, total - bound), min(bound, total - 1) + 1)
        return jnp.stack([one, total - one])
    sizes = jnp.asarray(profile(amount, total, bound, lean), jnp.int32)
    couples = (amount - 1) // 2
    source_of, taker = sizes[1:1 + 2 * couples:2], sizes[2:2 + 2 * couples:2]
    margin = jnp.minimum(source_of - 1, bound - taker)
    moved = jax.random.randint(jax.random.fold_in(stream_key, 1), (couples,), 0, 1 << 20) % (margin + 1)
    sizes = sizes.at[1:1 + 2 * couples:2].set(source_of - moved).at[2:2 + 2 * couples:2].set(taker + moved)
    return sizes[jax.random.permutation(jax.random.fold_in(stream_key, 2), amount)]


def noise(key, dims, spread, most, split=(), kind=jnp.bfloat16):
    array = spread * jax.random.normal(key, dims, jnp.float32)
    if split:
        array = array * level_of(key, dims, split, -0.22, 0.18)
    return jnp.clip(array, -most, most).astype(kind)


def setup_inputs(seed: int = 0) -> dict:
    key_of = jax.random.split(jax.random.key(seed), 13)
    return {
        "tokens": noise(key_of[0], (TOKENS, D), 1.0, 6.0, ((0, 32),)),
        "lengths": ragged_sizes(key_of[1], SEQS, SEQS * TOK_DEV * 3 // 4, TOK_DEV, 2).astype(jnp.int32),
        "in_weight": noise(key_of[2], (D, DPROJ), D ** -0.5, 0.125, ((0, 32),)),
        "out_weight": noise(key_of[3], (DIN, D), DIN ** -0.5, 0.09375, ((0, 32),)),
        "norm_gain": jnp.clip(1.0 + 0.1 * jax.random.normal(key_of[4], (D,), jnp.float32), 0.5, 1.5).astype(jnp.bfloat16),
        "conv_weight": noise(key_of[5], (CONV_CH, KCONV), KCONV ** -0.5, 3.0, ((0, 32),)),
        "conv_bias": jnp.clip(jax.random.uniform(key_of[6], (CONV_CH,), jnp.float32, -0.5, 0.5) * level_of(key_of[6], (CONV_CH,), ((0, 32),), -0.4, 0.0), -0.5, 0.5).astype(jnp.bfloat16),
        "out_gain": jnp.clip(1.0 + 0.1 * jax.random.normal(key_of[7], (DIN,), jnp.float32), 0.5, 1.5).astype(jnp.bfloat16),
        "a_log": jnp.clip(-3.0 + 4.6 * jax.random.uniform(key_of[8], (HEADS,), jnp.float32) ** level_of(key_of[8], (HEADS,), ((0, 8),), -0.2, 0.2), -3.0, 1.6),
        "dt_bias": jnp.clip(-6.0 + 3.0 * jax.random.uniform(key_of[9], (HEADS,), jnp.float32) ** level_of(key_of[9], (HEADS,), ((0, 8),), -0.2, 0.2), -6.0, -3.0),
        "d_skip": jnp.clip(0.5 + 1.0 * jax.random.uniform(key_of[10], (HEADS,), jnp.float32) ** level_of(key_of[10], (HEADS,), ((0, 8),), -0.2, 0.2), 0.5, 1.5),
        "cotangent": noise(key_of[11], (TOKENS, D), 1.0, 6.0, ((0, 32),)),
    }


EPS = 1e-05

@jax.custom_vjp
def low(v):
    return lax.optimization_barrier(v.astype(jnp.bfloat16)).astype(jnp.float32)

@jax.custom_vjp
def low_back(v):
    return v

def low_keep(v):
    return (low(v), None)

def low_pass(kept, grad):
    return (grad,)

def back_keep(v):
    return (v, None)

def back_low(kept, grad):
    return (low(grad),)
low.defvjp(low_keep, low_pass)
low_back.defvjp(back_keep, back_low)

def rms_scale(values, gain_vec):
    return values * lax.rsqrt(lax.optimization_barrier(jnp.mean(values * values, axis=-1, keepdims=True)) + EPS) * gain_vec

def block_step(carry_state, pieces, rounding):
    x_rows, b_rows, c_rows, dt_rows, log_decay = pieces
    block_len = x_rows.shape[0]
    head_count = dt_rows.shape[1]
    cum_decay = jnp.cumsum(log_decay, axis=0).T
    c_dot_b = jnp.dot(c_rows, b_rows.T, precision=lax.Precision.HIGHEST, preferred_element_type=jnp.float32)
    lower_mask = (lax.iota(jnp.int32, block_len)[:, None] >= lax.iota(jnp.int32, block_len)[None, :])[None]
    spread_log = cum_decay[:, :, None] - cum_decay[:, None, :]
    decays = jnp.where(lower_mask, jnp.exp(jnp.where(lower_mask, spread_log, 0.0)), 0.0)
    mixing = rounding(c_dot_b[None] * decays * dt_rows.T[:, None, :])
    x_heads = x_rows.reshape(block_len, head_count, -1)
    within = jnp.einsum('hts,shp->thp', mixing, x_heads, precision=lax.Precision.HIGHEST)
    carried = jnp.einsum('tn,hnp->thp', c_rows, carry_state, precision=lax.Precision.HIGHEST) * jnp.exp(cum_decay).T[:, :, None]
    end_decay = cum_decay[:, -1:]
    entry_scale = jnp.exp(end_decay - cum_decay) * dt_rows.T
    fresh_state = jnp.einsum('sn,hs,shp->hnp', b_rows, entry_scale, x_heads, precision=lax.Precision.HIGHEST)
    carry_state = carry_state * jnp.exp(end_decay)[:, :, None] + fresh_state
    return (carry_state, (within + carried).reshape(block_len, -1))

def ssd_mixer(projected, conv_w, conv_b, log_rate, rate_bias, skip_gain, gain_out, rounding):
    seq_len = projected.shape[0]
    inner_width = HEADS * HEAD_DIM
    channels = inner_width + 2 * NSTATE
    gate_part = projected[:, :inner_width]
    conv_in = projected[:, inner_width:inner_width + channels]
    dt_raw = projected[:, inner_width + channels:]
    padded = jnp.pad(conv_in, ((KCONV - 1, 0), (0, 0)))
    conv_out = conv_b
    for tap_idx in range(KCONV):
        conv_out = conv_out + padded[tap_idx:tap_idx + seq_len] * conv_w[:, tap_idx]
    active = jax.nn.silu(conv_out)
    x_rows = rounding(active[:, :inner_width])
    b_rows = rounding(active[:, inner_width:inner_width + NSTATE])
    c_rows = rounding(active[:, inner_width + NSTATE:])
    dt_rows = jax.nn.softplus(dt_raw + rate_bias)
    log_decay = -dt_rows * jnp.exp(log_rate)
    block_count = seq_len // SPAN

    def to_blocks(values):
        return values.reshape(block_count, SPAN, values.shape[1])
    zero_state = jnp.zeros((HEADS, NSTATE, HEAD_DIM), jnp.float32)
    _, block_outs = lax.scan(jax.checkpoint(partial(block_step, rounding=rounding)), zero_state, (to_blocks(x_rows), to_blocks(b_rows), to_blocks(c_rows), to_blocks(dt_rows), to_blocks(log_decay)))
    ssd_out = block_outs.reshape(seq_len, inner_width) + x_rows * jnp.repeat(skip_gain, HEAD_DIM)
    gated_out = ssd_out * jax.nn.silu(gate_part)
    return rms_scale(gated_out, gain_out)

def block_forward(tokens_f, in_w, out_w, gain_norm, conv_w, conv_b, gain_out, log_rate, rate_bias, skip_gain, live_mask):
    group_size = math.gcd(SEQS, max(1, 4096 // TOK_DEV))
    seq_rows = tokens_f.reshape(SEQS // group_size, group_size, TOK_DEV, D)
    seq_mask = live_mask.reshape(SEQS // group_size, group_size, TOK_DEV, 1)

    def one_seq(rows_in, mask_rows):
        normed = low(rms_scale(rows_in, gain_norm))
        projected = low_back(jnp.dot(normed, in_w, precision=lax.Precision.HIGHEST, preferred_element_type=jnp.float32))
        mixed = low(ssd_mixer(projected, conv_w, conv_b, log_rate, rate_bias, skip_gain, gain_out, low))
        branch = low_back(jnp.dot(mixed, out_w, precision=lax.Precision.HIGHEST, preferred_element_type=jnp.float32))
        return rows_in + mask_rows * branch

    def group_step(carry_val, pieces):
        return (carry_val, jax.vmap(one_seq)(pieces[0], pieces[1]))
    _, outs_all = lax.scan(jax.checkpoint(group_step), jnp.zeros((), jnp.float32), (seq_rows, seq_mask))
    return outs_all.reshape(TOKENS, D)

def reference(tokens, lengths, in_weight, out_weight, norm_gain, conv_weight, conv_bias, out_gain, a_log, dt_bias, d_skip, cotangent):
    positions = jnp.arange(TOK_DEV, dtype=jnp.int32)
    live_mask = (positions[None, :] < lengths.astype(jnp.int32)[:, None]).astype(jnp.float32).reshape(TOKENS, 1)
    primals = (tokens.astype(jnp.float32), in_weight.astype(jnp.float32), out_weight.astype(jnp.float32), norm_gain.astype(jnp.float32), conv_weight.astype(jnp.float32), conv_bias.astype(jnp.float32), out_gain.astype(jnp.float32), a_log.astype(jnp.float32), dt_bias.astype(jnp.float32), d_skip.astype(jnp.float32))

    def run_block(*values):
        return block_forward(*values, live_mask)
    output, pull_back = jax.vjp(run_block, *primals)
    grads = pull_back(cotangent.astype(jnp.float32))
    return (output.astype(jnp.bfloat16), grads[0].astype(jnp.bfloat16), grads[1], grads[2], grads[3], grads[4], grads[5], grads[6], grads[7], grads[8], grads[9])
```

```python
from functools import partial

import jax
import jax.numpy as jnp
from jax import lax
from jax.sharding import PartitionSpec as P

HEADS = 64
HEAD_DIM = 64
NSTATE = 128
KCONV = 4
SPAN = 256


EPS = 1e-05


def rounded(values):
    fixed = lax.stop_gradient(values)
    coarse = lax.optimization_barrier(fixed.astype(jnp.bfloat16)).astype(jnp.float32)
    return values + (coarse - fixed)


def rms_scale(values, gain_vec):
    return values * lax.rsqrt(jnp.mean(values * values, axis=-1, keepdims=True) + EPS) * gain_vec


def block_step(carry_state, pieces, rounding):
    x_rows, b_rows, c_rows, dt_rows, log_decay = pieces
    block_len = x_rows.shape[0]
    head_count = dt_rows.shape[1]
    cum_decay = jnp.cumsum(log_decay, axis=0).T
    c_dot_b = jnp.dot(c_rows, b_rows.T, preferred_element_type=jnp.float32)
    lower_mask = (
        lax.iota(jnp.int32, block_len)[:, None] >= lax.iota(jnp.int32, block_len)[None, :]
    )[None]
    spread_log = cum_decay[:, :, None] - cum_decay[:, None, :]
    decays = jnp.where(lower_mask, jnp.exp(jnp.where(lower_mask, spread_log, 0.0)), 0.0)
    mixing = rounding(c_dot_b[None] * decays * dt_rows.T[:, None, :])
    x_heads = x_rows.reshape(block_len, head_count, -1)
    within = jnp.einsum("hts,shp->thp", mixing, x_heads, preferred_element_type=jnp.float32)
    carried = (
        jnp.einsum("tn,hnp->thp", c_rows, carry_state, preferred_element_type=jnp.float32)
        * jnp.exp(cum_decay).T[:, :, None]
    )
    end_decay = cum_decay[:, -1:]
    entry_scale = jnp.exp(end_decay - cum_decay) * dt_rows.T
    fresh_state = jnp.einsum(
        "sn,hs,shp->hnp", b_rows, entry_scale, x_heads, preferred_element_type=jnp.float32
    )
    carry_state = carry_state * jnp.exp(end_decay)[:, :, None] + fresh_state
    return (carry_state, (within + carried).reshape(block_len, -1))


def ssd_mixer(projected, conv_w, conv_b, log_rate, rate_bias, skip_gain, gain_out, rounding):
    seq_len = projected.shape[0]
    inner_width = HEADS * HEAD_DIM
    channels = inner_width + 2 * NSTATE
    gate_part = projected[:, :inner_width]
    conv_in = projected[:, inner_width : inner_width + channels]
    dt_raw = projected[:, inner_width + channels :]
    padded = jnp.pad(conv_in, ((KCONV - 1, 0), (0, 0)))
    conv_out = conv_b
    for tap_idx in range(KCONV):
        conv_out = conv_out + padded[tap_idx : tap_idx + seq_len] * conv_w[:, tap_idx]
    active = jax.nn.silu(conv_out)
    x_rows = rounding(active[:, :inner_width])
    b_rows = rounding(active[:, inner_width : inner_width + NSTATE])
    c_rows = rounding(active[:, inner_width + NSTATE :])
    dt_rows = jax.nn.softplus(dt_raw + rate_bias)
    log_decay = -dt_rows * jnp.exp(log_rate)
    block_count = seq_len // SPAN

    def to_blocks(values):
        return values.reshape(block_count, SPAN, values.shape[1])

    zero_state = jnp.zeros((HEADS, NSTATE, HEAD_DIM), jnp.float32)
    _, block_outs = lax.scan(
        jax.checkpoint(partial(block_step, rounding=rounding)),
        zero_state,
        (
            to_blocks(x_rows),
            to_blocks(b_rows),
            to_blocks(c_rows),
            to_blocks(dt_rows),
            to_blocks(log_decay),
        ),
    )
    ssd_out = block_outs.reshape(seq_len, inner_width) + x_rows * jnp.repeat(skip_gain, HEAD_DIM)
    gated_out = ssd_out * jax.nn.silu(gate_part)
    return rms_scale(gated_out, gain_out)


def fetch_weights(in_part, out_part, norm_part, conv_part, bias_part, gain_part):
    return (
        lax.all_gather(in_part, ("wide", "narrow"), axis=0, tiled=True),
        lax.all_gather(out_part, ("wide", "narrow"), axis=0, tiled=True),
        lax.all_gather(norm_part, ("wide", "narrow"), axis=0, tiled=True),
        lax.all_gather(conv_part, ("wide", "narrow"), axis=0, tiled=True),
        lax.all_gather(bias_part, ("wide", "narrow"), axis=0, tiled=True),
        lax.all_gather(gain_part, ("wide", "narrow"), axis=0, tiled=True),
    )


def spread_heads(head_grad, wide_count, narrow_count):
    share_len = head_grad.shape[0] // wide_count
    blocks = jnp.broadcast_to(
        head_grad.reshape(wide_count, 1, share_len), (wide_count, narrow_count, share_len)
    )
    return blocks.reshape(-1)


def settle_grads(
    normed_low,
    proj_grad,
    mixed_low,
    branch_grad,
    norm_term,
    conv_term,
    bias_term,
    gain_term,
    head_terms,
):
    wide_count = lax.axis_size("wide")
    narrow_count = lax.axis_size("narrow")
    heads_laid = [spread_heads(head_term, wide_count, narrow_count) for head_term in head_terms]
    columns = normed_low
    inw_own = lax.psum_scatter(
        lax.dot_general(
            columns, proj_grad, (((0,), (0,)), ((), ())), preferred_element_type=jnp.float32
        ).astype(jnp.bfloat16),
        ("wide", "narrow"),
        scatter_dimension=0,
        tiled=True,
    ).astype(jnp.float32)
    columns = mixed_low
    outw_own = lax.psum_scatter(
        lax.dot_general(
            columns, branch_grad, (((0,), (0,)), ((), ())), preferred_element_type=jnp.float32
        ).astype(jnp.bfloat16),
        ("wide", "narrow"),
        scatter_dimension=0,
        tiled=True,
    ).astype(jnp.float32)
    small_own = (
        lax.psum_scatter(norm_term, ("wide", "narrow"), scatter_dimension=0, tiled=True),
        lax.psum_scatter(conv_term, ("wide", "narrow"), scatter_dimension=0, tiled=True),
        lax.psum_scatter(bias_term, ("wide", "narrow"), scatter_dimension=0, tiled=True),
        lax.psum_scatter(gain_term, ("wide", "narrow"), scatter_dimension=0, tiled=True),
        lax.psum_scatter(heads_laid[0], ("wide", "narrow"), scatter_dimension=0, tiled=True),
        lax.psum_scatter(heads_laid[1], ("wide", "narrow"), scatter_dimension=0, tiled=True),
        lax.psum_scatter(heads_laid[2], ("wide", "narrow"), scatter_dimension=0, tiled=True),
    )
    return (inw_own, outw_own) + tuple(small_own)


def body(
    tokens,
    lengths,
    in_weight,
    out_weight,
    norm_gain,
    conv_weight,
    conv_bias,
    out_gain,
    a_log,
    dt_bias,
    d_skip,
    cotangent,
):
    row_count = tokens.shape[0]
    live_mask = (lax.iota(jnp.int32, row_count) < lengths[0]).astype(jnp.float32)[:, None]
    gathered = fetch_weights(in_weight, out_weight, norm_gain, conv_weight, conv_bias, out_gain)
    head_values = (
        lax.all_gather(a_log, "wide", axis=0, tiled=True),
        lax.all_gather(dt_bias, "wide", axis=0, tiled=True),
        lax.all_gather(d_skip, "wide", axis=0, tiled=True),
    )
    source = tokens.astype(jnp.float32)
    normed, front_back = jax.vjp(rms_scale, source, gathered[2].astype(jnp.float32))
    normed_low = normed.astype(jnp.bfloat16)
    projected = jnp.dot(normed_low, gathered[0], preferred_element_type=jnp.float32)

    def mix_local(proj_rows, conv_w, conv_b, log_rate, rate_bias, skip_gain, gain_out):
        return ssd_mixer(
            proj_rows, conv_w, conv_b, log_rate, rate_bias, skip_gain, gain_out, rounded
        )

    mixed, mix_back = jax.vjp(
        mix_local,
        projected,
        gathered[3].astype(jnp.float32),
        gathered[4].astype(jnp.float32),
        head_values[0],
        head_values[1],
        head_values[2],
        gathered[5].astype(jnp.float32),
    )
    mixed_low = mixed.astype(jnp.bfloat16)
    branch = jnp.dot(mixed_low, gathered[1], preferred_element_type=jnp.float32)
    output = (source + live_mask * branch).astype(jnp.bfloat16)
    gathered = fetch_weights(in_weight, out_weight, norm_gain, conv_weight, conv_bias, out_gain)
    cot_rows = cotangent.astype(jnp.float32)
    branch_grad = (live_mask * cot_rows).astype(jnp.bfloat16)
    mixed_grad = lax.dot_general(
        branch_grad, gathered[1], (((1,), (1,)), ((), ())), preferred_element_type=jnp.float32
    )
    mix_grads = mix_back(mixed_grad)
    proj_grad = mix_grads[0].astype(jnp.bfloat16)
    normed_grad = lax.dot_general(
        proj_grad, gathered[0], (((1,), (1,)), ((), ())), preferred_element_type=jnp.float32
    )
    source_grad, normgain_grad = front_back(normed_grad)
    token_grad = (cot_rows + source_grad).astype(jnp.bfloat16)
    owned = settle_grads(
        normed_low,
        proj_grad,
        mixed_low,
        branch_grad,
        normgain_grad,
        mix_grads[1],
        mix_grads[2],
        mix_grads[6],
        (mix_grads[3], mix_grads[4], mix_grads[5]),
    )
    return (
        output,
        token_grad,
        owned[0],
        owned[1],
        owned[2],
        owned[3],
        owned[4],
        owned[5],
        owned[6],
        owned[7],
        owned[8],
    )


def solution(mesh):
    in_specs = (
        P(("wide", "narrow"), None),
        P(("wide", "narrow")),
        P(("wide", "narrow"), None),
        P(("wide", "narrow"), None),
        P(("wide", "narrow")),
        P(("wide", "narrow"), None),
        P(("wide", "narrow")),
        P(("wide", "narrow")),
        P("wide"),
        P("wide"),
        P("wide"),
        P(("wide", "narrow"), None),
    )
    out_specs = (
        P(("wide", "narrow"), None),
        P(("wide", "narrow"), None),
        P(("wide", "narrow"), None),
        P(("wide", "narrow"), None),
        P(("wide", "narrow")),
        P(("wide", "narrow"), None),
        P(("wide", "narrow")),
        P(("wide", "narrow")),
        P("wide"),
        P("wide"),
        P("wide"),
    )
    return jax.shard_map(body, mesh=mesh, in_specs=in_specs, out_specs=out_specs, check_vma=False)
```

```python
import jax
import jax.numpy as jnp
from jax import lax
from jax.experimental import pallas as pl
from jax.experimental.pallas import tpu as pltpu
from jax.sharding import PartitionSpec as P

HEADS = 64
HEAD_DIM = 64
NSTATE = 128
KCONV = 4
DIN = HEADS * HEAD_DIM
CHUNK = 128
GROUP = 256
NEVER = -1e30


EPS = 1e-05


def silu_parts(values):
    gate = 1.0 / (1.0 + jnp.exp(-values))
    return gate, values * gate


def mm(left, right):
    return lax.dot_general(left, right, (((1,), (0,)), ((), ())), preferred_element_type=jnp.float32)


def mm_nt(left, right):
    return lax.dot_general(left, right, (((1,), (1,)), ((), ())), preferred_element_type=jnp.float32)


def mm_tn(left, right):
    return lax.dot_general(left, right, (((0,), (0,)), ((), ())), preferred_element_type=jnp.float32)


def low16(values):
    return values.astype(jnp.bfloat16)


def tile_masks():
    row_id = lax.broadcasted_iota(jnp.int32, (CHUNK, CHUNK), 0)
    col_id = lax.broadcasted_iota(jnp.int32, (CHUNK, CHUNK), 1)
    return row_id >= col_id, col_id < HEAD_DIM


def conv_tile(pad_ref, par_ref, start, lanes):
    total = par_ref[4:5, lanes]
    for tap in range(KCONV):
        first = start + 8 - (KCONV - 1) + tap
        total = total + pad_ref[first : first + CHUNK, lanes] * par_ref[tap : tap + 1, lanes]
    return total


def fill_pad(pad_ref, source_ref):
    pad_ref[0:8, :] = jnp.zeros((8, GROUP), jnp.float32)
    pad_ref[8:, :] = source_ref[...]


def ssd_forward_kernel(
    xin_ref, z_ref, par_ref, b_ref, c_ref, bt_ref, dtc_ref, cumc_ref, dtr_ref, cumr_ref,
    x_ref, y_ref, s_ref, ssq_ref, pad_ref,
):
    rows = xin_ref.shape[0]
    causal, first_head = tile_masks()
    fill_pad(pad_ref, xin_ref)

    @pl.when(pl.program_id(1) == 0)
    def _():
        ssq_ref[...] = jnp.zeros(ssq_ref.shape, jnp.float32)

    for pair in range(GROUP // 128):
        lanes = slice(pair * 128, pair * 128 + 128)
        state = None
        for q in range(rows // CHUNK):
            span = slice(q * CHUNK, q * CHUNK + CHUNK)
            c_dot_b = mm_nt(c_ref[span, :], b_ref[span, :])
            _, active = silu_parts(conv_tile(pad_ref, par_ref, q * CHUNK, lanes))
            x_low = low16(active)
            x_ref[span, lanes] = x_low
            x_wide = x_low.astype(jnp.float32)
            within, cums, dts, ends = [], [], [], []
            for sub in range(2):
                head = pair * 2 + sub
                col = cumc_ref[0, span, head : head + 1]
                row = cumr_ref[0, head : head + 1, span]
                dt_row = dtr_ref[0, head : head + 1, span]
                decay = jnp.exp(jnp.where(causal, col - row, NEVER))
                within.append(mm(low16(c_dot_b * decay * dt_row), x_low))
                cums.append(col)
                dts.append(dtc_ref[0, span, head : head + 1])
                ends.append(cumc_ref[0, q * CHUNK + CHUNK - 1 : q * CHUNK + CHUNK, head : head + 1])
            out = jnp.where(first_head, within[0], within[1]) + par_ref[5:6, lanes] * x_wide
            if q:
                s_ref[q - 1, :, lanes] = low16(state)
                entry = jnp.where(first_head, jnp.exp(cums[0]), jnp.exp(cums[1]))
                out = out + entry * mm(c_ref[span, :], low16(state))
            y_ref[span, lanes] = out
            _, gate = silu_parts(z_ref[span, lanes])
            gated = out * gate
            ssq_ref[span, :] += gated * gated
            if q + 1 < rows // CHUNK:
                weight = jnp.where(
                    first_head, jnp.exp(ends[0] - cums[0]) * dts[0], jnp.exp(ends[1] - cums[1]) * dts[1]
                )
                fresh = mm(bt_ref[:, span], low16(x_wide * weight))
                if q:
                    fresh = fresh + state * jnp.where(first_head, jnp.exp(ends[0]), jnp.exp(ends[1]))
                state = fresh


def ssd_backward_kernel(
    xin_ref, z_ref, par_ref, b_ref, c_ref, ct_ref, dtc_ref, cumc_ref, dtr_ref, cumr_ref,
    x_ref, y_ref, s_ref, mg_ref, rc_ref,
    zg_ref, xg_ref, pg_ref, gb_ref, gc_ref, rv_ref, u_ref, e_ref,
    pad_ref, gpad_ref, gcb_ref,
):
    rows = xin_ref.shape[0]
    count = rows // CHUNK
    causal, first_head = tile_masks()
    lane_id = lax.broadcasted_iota(jnp.int32, (CHUNK, 128), 1)
    fill_pad(pad_ref, xin_ref)
    gpad_ref[rows:, :] = jnp.zeros((8, GROUP), jnp.float32)

    @pl.when(pl.program_id(1) == 0)
    def _():
        gb_ref[...] = jnp.zeros(gb_ref.shape, jnp.float32)
        gc_ref[...] = jnp.zeros(gc_ref.shape, jnp.float32)
        gcb_ref[...] = jnp.zeros(gcb_ref.shape, jnp.float32)

    columns = [jnp.zeros((CHUNK, 128), jnp.float32) for _ in range(count)]
    for pair in range(GROUP // 128):
        lanes = slice(pair * 128, pair * 128 + 128)
        state_grad = None
        sums = [jnp.zeros((1, 128), jnp.float32) for _ in range(7)]
        for q in reversed(range(count)):
            span = slice(q * CHUNK, q * CHUNK + CHUNK)
            b_low, c_low = b_ref[span, :], c_ref[span, :]
            c_dot_b = mm_nt(c_low, b_low)
            z_tile, y_tile, mg_tile = z_ref[span, lanes], y_ref[span, lanes], mg_ref[span, lanes]
            scale, coef = rc_ref[span, 0:1], rc_ref[span, 1:2]
            gate_sig, gate = silu_parts(z_tile)
            gated = y_tile * gate
            scaled = scale * mg_tile
            gated_grad = scaled * par_ref[6:7, lanes] - gated * coef
            zg_ref[span, lanes] = low16(
                gated_grad * y_tile * (gate_sig * (1.0 + z_tile * (1.0 - gate_sig)))
            )
            grad = gated_grad * gate
            grad_low = low16(grad)
            x_low = x_ref[span, lanes]
            x_wide = x_low.astype(jnp.float32)
            sums[6] += jnp.sum(gated * scaled, axis=0, keepdims=True)
            sums[5] += jnp.sum(grad * x_wide, axis=0, keepdims=True)
            cums, ends = [], []
            for sub in range(2):
                head = pair * 2 + sub
                cums.append(cumc_ref[0, span, head : head + 1])
                ends.append(cumc_ref[0, q * CHUNK + CHUNK - 1 : q * CHUNK + CHUNK, head : head + 1])
            entry = jnp.where(first_head, jnp.exp(cums[0]), jnp.exp(cums[1]))
            carried = jnp.zeros((CHUNK, 128), jnp.float32)
            entered = low16(grad * entry)
            if q:
                s_low = s_ref[q - 1, :, lanes]
                carried = grad * entry * mm(c_low, s_low)
                gc_ref[span, :] += mm_nt(entered, s_low)
            x_grad = par_ref[5:6, lanes] * grad
            leaving = None
            if state_grad is not None:
                sg_low = low16(state_grad)
                late = jnp.where(first_head, jnp.exp(ends[0] - cums[0]), jnp.exp(ends[1] - cums[1]))
                dt_cols = [dtc_ref[0, span, pair * 2 + sub : pair * 2 + sub + 1] for sub in range(2)]
                weight = late * jnp.where(first_head, dt_cols[0], dt_cols[1])
                b_state = mm(b_low, sg_low)
                x_grad = x_grad + weight * b_state
                leaving = late * x_wide * b_state
                gb_ref[span, :] += mm_nt(low16(x_wide * weight), sg_low)
            for sub in range(2):
                head = pair * 2 + sub
                mine = first_head if sub == 0 else jnp.logical_not(first_head)
                row = cumr_ref[0, head : head + 1, span]
                dt_row = dtr_ref[0, head : head + 1, span]
                decay = jnp.exp(jnp.where(causal, cums[sub] - row, NEVER))
                grad_mine = jnp.where(mine, grad_low, jnp.zeros_like(grad_low))
                mix_grad = mm_nt(grad_mine, x_low) * decay
                x_grad = x_grad + mm_tn(low16(c_dot_b * decay * dt_row), grad_mine)
                gcb_ref[span, :] += mix_grad * dt_row
                direct = mix_grad * c_dot_b
                u_ref[0, head : head + 1, span] = jnp.sum(direct, axis=0, keepdims=True)
                total = direct * dt_row + jnp.where(mine, carried, 0.0)
                columns[q] = jnp.where(
                    lane_id == head, jnp.sum(total, axis=1, keepdims=True), columns[q]
                )
                if leaving is not None:
                    columns[q] = jnp.where(
                        lane_id == head + GROUP // HEAD_DIM,
                        jnp.sum(jnp.where(mine, leaving, 0.0), axis=1, keepdims=True),
                        columns[q],
                    )
            pre = conv_tile(pad_ref, par_ref, q * CHUNK, lanes)
            pre_sig, _ = silu_parts(pre)
            pre_grad = x_grad * (pre_sig * (1.0 + pre * (1.0 - pre_sig)))
            gpad_ref[span, lanes] = pre_grad
            sums[4] += jnp.sum(pre_grad, axis=0, keepdims=True)
            back = jnp.zeros((CHUNK, 128), jnp.float32)
            for tap in range(KCONV):
                first = q * CHUNK + 8 - (KCONV - 1) + tap
                sums[tap] += jnp.sum(pre_grad * pad_ref[first : first + CHUNK, lanes], axis=0, keepdims=True)
                ahead = q * CHUNK + KCONV - 1 - tap
                back = back + gpad_ref[ahead : ahead + CHUNK, lanes] * par_ref[tap : tap + 1, lanes]
            xg_ref[span, lanes] = low16(back)
            end_scale = jnp.where(first_head, jnp.exp(ends[0]), jnp.exp(ends[1]))[0:1, :]
            if q and state_grad is not None:
                e_ref[0, q : q + 1, lanes] = end_scale * jnp.sum(
                    s_low.astype(jnp.float32) * state_grad, axis=0, keepdims=True
                )
            else:
                e_ref[0, q : q + 1, lanes] = jnp.zeros((1, 128), jnp.float32)
            if q:
                fresh = mm(ct_ref[:, span], entered)
                state_grad = fresh if state_grad is None else fresh + end_scale * state_grad
        for index in range(7):
            pg_ref[0, index : index + 1, lanes] = sums[index]
        pg_ref[0, 7:8, lanes] = jnp.zeros((1, 128), jnp.float32)
    for q in range(count):
        rv_ref[0, q * CHUNK : q * CHUNK + CHUNK, :] = columns[q]

    @pl.when(pl.program_id(1) == pl.num_programs(1) - 1)
    def _():
        for q in range(count):
            span = slice(q * CHUNK, q * CHUNK + CHUNK)
            joint = low16(gcb_ref[span, :])
            gc_ref[span, :] += mm(joint, b_ref[span, :])
            gb_ref[span, :] += mm_tn(joint, c_ref[span, :])


def wide_spec(rows, offset=0):
    return pl.BlockSpec((rows, GROUP), lambda i, g: (i, g + offset))


def shared_specs(rows, per, groups):
    row_spec = pl.BlockSpec((rows, NSTATE), lambda i, g: (i, 0))
    return [
        pl.BlockSpec((8, GROUP), lambda i, g: (0, g)),
        row_spec,
        row_spec,
        pl.BlockSpec((NSTATE, rows), lambda i, g: (0, i)),
        pl.BlockSpec((1, rows, per), lambda i, g: (g, i, 0)),
        pl.BlockSpec((1, rows, per), lambda i, g: (g, i, 0)),
        pl.BlockSpec((1, per, rows), lambda i, g: (g, 0, i)),
        pl.BlockSpec((1, per, rows), lambda i, g: (g, 0, i)),
    ]


def ssd_forward(proj, x_at, z_at, par, b_low, c_low, forms, rows):
    width = par.shape[1]
    seqs, groups, per = proj.shape[0] // rows, width // GROUP, GROUP // HEAD_DIM
    total = seqs * rows
    steps = rows // CHUNK
    return pl.pallas_call(
        ssd_forward_kernel,
        grid=(seqs, groups),
        in_specs=[wide_spec(rows, x_at), wide_spec(rows, z_at)] + shared_specs(rows, per, groups),
        out_specs=[
            wide_spec(rows),
            wide_spec(rows),
            pl.BlockSpec((steps - 1, NSTATE, GROUP), lambda i, g: (i, 0, g)),
            pl.BlockSpec((rows, 128), lambda i, g: (i, 0)),
        ],
        out_shape=[
            jax.ShapeDtypeStruct((total, width), jnp.bfloat16),
            jax.ShapeDtypeStruct((total, width), jnp.float32),
            jax.ShapeDtypeStruct((seqs * (steps - 1), NSTATE, width), jnp.bfloat16),
            jax.ShapeDtypeStruct((total, 128), jnp.float32),
        ],
        scratch_shapes=[pltpu.VMEM((rows + 8, GROUP), jnp.float32)],
        compiler_params=pltpu.CompilerParams(dimension_semantics=("arbitrary", "arbitrary")),
        name="ssd_forward",
    )(proj, proj, par, b_low, c_low, b_low.T, *forms)


def ssd_backward(proj, x_at, z_at, par, b_low, c_low, forms, x_low, y, states, mixed_grad, row_coef, rows):
    width = par.shape[1]
    seqs, groups, per = proj.shape[0] // rows, width // GROUP, GROUP // HEAD_DIM
    total = seqs * rows
    steps = rows // CHUNK
    return pl.pallas_call(
        ssd_backward_kernel,
        grid=(seqs, groups),
        in_specs=[wide_spec(rows, x_at), wide_spec(rows, z_at)]
        + shared_specs(rows, per, groups)
        + [
            wide_spec(rows),
            wide_spec(rows),
            pl.BlockSpec((steps - 1, NSTATE, GROUP), lambda i, g: (i, 0, g)),
            wide_spec(rows),
            pl.BlockSpec((rows, 2), lambda i, g: (i, 0)),
        ],
        out_specs=[
            wide_spec(rows),
            wide_spec(rows),
            pl.BlockSpec((1, 8, GROUP), lambda i, g: (i, 0, g)),
            pl.BlockSpec((rows, NSTATE), lambda i, g: (i, 0)),
            pl.BlockSpec((rows, NSTATE), lambda i, g: (i, 0)),
            pl.BlockSpec((1, rows, 128), lambda i, g: (g, i, 0)),
            pl.BlockSpec((1, per, rows), lambda i, g: (g, 0, i)),
            pl.BlockSpec((1, steps, GROUP), lambda i, g: (i, 0, g)),
        ],
        out_shape=[
            jax.ShapeDtypeStruct((total, width), jnp.bfloat16),
            jax.ShapeDtypeStruct((total, width), jnp.bfloat16),
            jax.ShapeDtypeStruct((seqs, 8, width), jnp.float32),
            jax.ShapeDtypeStruct((total, NSTATE), jnp.float32),
            jax.ShapeDtypeStruct((total, NSTATE), jnp.float32),
            jax.ShapeDtypeStruct((groups, total, 128), jnp.float32),
            jax.ShapeDtypeStruct((groups, per, total), jnp.float32),
            jax.ShapeDtypeStruct((seqs, steps, width), jnp.float32),
        ],
        scratch_shapes=[
            pltpu.VMEM((rows + 8, GROUP), jnp.float32),
            pltpu.VMEM((rows + 8, GROUP), jnp.float32),
            pltpu.VMEM((rows, CHUNK), jnp.float32),
        ],
        compiler_params=pltpu.CompilerParams(dimension_semantics=("arbitrary", "arbitrary")),
        name="ssd_backward",
    )(proj, proj, par, b_low, c_low, c_low.T, *forms, x_low, y, states, mixed_grad, row_coef)


def conv_small(values, taps, bias, rows):
    seqs = values.shape[0] // rows
    padded = jnp.pad(values.reshape(seqs, rows, -1), ((0, 0), (KCONV - 1, 0), (0, 0)))
    total = bias
    for tap in range(KCONV):
        total = total + padded[:, tap : tap + rows] * taps[tap]
    return total.reshape(seqs * rows, -1)


def conv_small_back(grad, values, taps, rows):
    seqs = values.shape[0] // rows
    padded = jnp.pad(values.reshape(seqs, rows, -1), ((0, 0), (KCONV - 1, 0), (0, 0)))
    ahead = jnp.pad(grad.reshape(seqs, rows, -1), ((0, 0), (0, KCONV - 1), (0, 0)))
    grads = grad.reshape(seqs, rows, -1)
    back = 0.0
    tap_grads = []
    for tap in range(KCONV):
        shift = KCONV - 1 - tap
        back = back + ahead[:, shift : shift + rows] * taps[tap]
        tap_grads.append(jnp.sum(grads * padded[:, tap : tap + rows], axis=(0, 1)))
    return back.reshape(values.shape), jnp.stack(tap_grads), jnp.sum(grad, axis=0)


def chunk_sums(values, lower):
    size = values.shape[0]
    shape = (CHUNK, CHUNK)
    before = lax.broadcasted_iota(jnp.int32, shape, 0) >= lax.broadcasted_iota(jnp.int32, shape, 1)
    kernel = (before if lower else before.T).astype(jnp.float32)
    return jnp.einsum(
        "ts,qsh->qth", kernel, values.reshape(size // CHUNK, CHUNK, -1), precision=lax.Precision.HIGHEST
    ).reshape(values.shape)


def head_forms(dt_rows, cum):
    per = GROUP // HEAD_DIM
    size, heads = dt_rows.shape

    def by_col(values):
        return values.reshape(size, heads // per, per).transpose(1, 0, 2)

    def by_row(values):
        return values.T.reshape(heads // per, per, size)

    return by_col(dt_rows), by_col(cum), by_row(dt_rows), by_row(cum)


def heads_back(rv, u, e, dt_rows, log_decay, rate, rows):
    per = GROUP // HEAD_DIM
    size, heads = dt_rows.shape
    row_term = rv[:, :, :per].transpose(1, 0, 2).reshape(size, heads)
    leave = rv[:, :, per : 2 * per].transpose(1, 0, 2).reshape(size, heads)
    direct = u.reshape(heads, size).T + leave
    cum_grad = row_term - dt_rows * direct
    ends = jnp.sum((dt_rows * leave).reshape(size // CHUNK, CHUNK, heads), axis=1)
    ends = ends + jnp.sum(e.reshape(size // CHUNK, heads, HEAD_DIM), axis=2)
    log_grad = chunk_sums(cum_grad, False).reshape(size // CHUNK, CHUNK, heads) + ends[:, None, :]
    log_grad = log_grad.reshape(size, heads)
    dt_grad = direct - log_grad * rate
    return dt_grad, jnp.sum(log_grad * log_decay, axis=0)


def rms_scale(values, gain_vec):
    return values * lax.rsqrt(jnp.mean(values * values, axis=-1, keepdims=True) + EPS) * gain_vec


def prepare(proj, x_at, conv_w, conv_b, a_log, dt_bias, rows):
    small = proj[:, x_at + DIN :]
    taps = conv_w[DIN:].T
    pre = conv_small(small[:, : 2 * NSTATE], taps, conv_b[DIN:], rows)
    low = low16(pre * jax.nn.sigmoid(pre))
    dt_pre = small[:, 2 * NSTATE :] + dt_bias
    dt_rows = jax.nn.softplus(dt_pre)
    log_decay = -dt_rows * jnp.exp(a_log)
    forms = head_forms(dt_rows, chunk_sums(log_decay, True))
    return small[:, : 2 * NSTATE], pre, low[:, :NSTATE], low[:, NSTATE:], dt_pre, dt_rows, log_decay, forms


def fetch_weights(in_part, out_part, norm_part, conv_part, bias_part, gain_part):
    return (
        lax.all_gather(in_part, ("wide", "narrow"), axis=0, tiled=True),
        lax.all_gather(out_part, ("wide", "narrow"), axis=0, tiled=True),
        lax.all_gather(norm_part, ("wide", "narrow"), axis=0, tiled=True),
        lax.all_gather(conv_part, ("wide", "narrow"), axis=0, tiled=True),
        lax.all_gather(bias_part, ("wide", "narrow"), axis=0, tiled=True),
        lax.all_gather(gain_part, ("wide", "narrow"), axis=0, tiled=True),
    )


def spread_heads(head_grad, wide_count, narrow_count):
    share_len = head_grad.shape[0] // wide_count
    blocks = jnp.broadcast_to(
        head_grad.reshape(wide_count, 1, share_len), (wide_count, narrow_count, share_len)
    )
    return blocks.reshape(-1)


def settle_grads(
    normed_low,
    proj_grad,
    mixed_low,
    branch_grad,
    norm_term,
    conv_term,
    bias_term,
    gain_term,
    head_terms,
):
    wide_count = lax.axis_size("wide")
    narrow_count = lax.axis_size("narrow")
    heads_laid = [spread_heads(head_term, wide_count, narrow_count) for head_term in head_terms]
    columns = normed_low
    inw_own = lax.psum_scatter(
        lax.dot_general(
            columns, proj_grad, (((0,), (0,)), ((), ())), preferred_element_type=jnp.float32
        ).astype(jnp.bfloat16),
        ("wide", "narrow"),
        scatter_dimension=0,
        tiled=True,
    ).astype(jnp.float32)
    columns = mixed_low
    outw_own = lax.psum_scatter(
        lax.dot_general(
            columns, branch_grad, (((0,), (0,)), ((), ())), preferred_element_type=jnp.float32
        ).astype(jnp.bfloat16),
        ("wide", "narrow"),
        scatter_dimension=0,
        tiled=True,
    ).astype(jnp.float32)
    small_own = (
        lax.psum_scatter(norm_term, ("wide", "narrow"), scatter_dimension=0, tiled=True),
        lax.psum_scatter(conv_term, ("wide", "narrow"), scatter_dimension=0, tiled=True),
        lax.psum_scatter(bias_term, ("wide", "narrow"), scatter_dimension=0, tiled=True),
        lax.psum_scatter(gain_term, ("wide", "narrow"), scatter_dimension=0, tiled=True),
        lax.psum_scatter(heads_laid[0], ("wide", "narrow"), scatter_dimension=0, tiled=True),
        lax.psum_scatter(heads_laid[1], ("wide", "narrow"), scatter_dimension=0, tiled=True),
        lax.psum_scatter(heads_laid[2], ("wide", "narrow"), scatter_dimension=0, tiled=True),
    )
    return (inw_own, outw_own) + tuple(small_own)


def body(
    tokens,
    lengths,
    in_weight,
    out_weight,
    norm_gain,
    conv_weight,
    conv_bias,
    out_gain,
    a_log,
    dt_bias,
    d_skip,
    cotangent,
):
    row_count = tokens.shape[0]
    live_mask = (lax.iota(jnp.int32, row_count) < lengths[0]).astype(jnp.float32)[:, None]
    gathered = fetch_weights(in_weight, out_weight, norm_gain, conv_weight, conv_bias, out_gain)
    head_values = (
        lax.all_gather(a_log, "wide", axis=0, tiled=True),
        lax.all_gather(dt_bias, "wide", axis=0, tiled=True),
        lax.all_gather(d_skip, "wide", axis=0, tiled=True),
    )
    source = tokens.astype(jnp.float32)
    normed, front_back = jax.vjp(rms_scale, source, gathered[2].astype(jnp.float32))
    normed_low = normed.astype(jnp.bfloat16)
    projected = jnp.dot(normed_low, gathered[0], preferred_element_type=jnp.float32)

    conv_w, conv_b = gathered[3].astype(jnp.float32), gathered[4].astype(jnp.float32)
    gain_out = gathered[5].astype(jnp.float32)
    a_full, bias_full, skip_full = head_values
    par = jnp.concatenate(
        [
            conv_w[:DIN].T,
            conv_b[None, :DIN],
            jnp.repeat(skip_full, HEAD_DIM)[None],
            gain_out[None],
            jnp.zeros((1, DIN), jnp.float32),
        ]
    )
    bc_in, bc_pre, b_low, c_low, dt_pre, dt_rows, log_decay, forms = prepare(
        projected, DIN, conv_w, conv_b, a_full, bias_full, row_count
    )
    x_block, z_block = DIN // GROUP, 0
    x_low, y, states, ssq = ssd_forward(
        projected, x_block, z_block, par, b_low, c_low, forms, row_count
    )
    z_part = projected[:, :DIN]
    gated = y * (z_part * jax.nn.sigmoid(z_part))
    inverse = lax.rsqrt(jnp.sum(ssq, axis=1, keepdims=True) / DIN + EPS)
    mixed_low = low16(gated * inverse * gain_out)
    branch = jnp.dot(mixed_low, gathered[1], preferred_element_type=jnp.float32)
    output = (source + live_mask * branch).astype(jnp.bfloat16)
    cot_rows = cotangent.astype(jnp.float32)
    branch_grad = (live_mask * cot_rows).astype(jnp.bfloat16)
    mixed_grad = lax.dot_general(
        branch_grad, gathered[1], (((1,), (1,)), ((), ())), preferred_element_type=jnp.float32
    )
    row_dot = jnp.sum(gated * gain_out * mixed_grad, axis=1, keepdims=True)
    row_coef = jnp.concatenate([inverse, inverse * inverse * inverse * row_dot / DIN], axis=1)
    z_grad, x_grad, par_grad, b_grad, c_grad, rv, u, e = ssd_backward(
        projected, x_block, z_block, par, b_low, c_low, forms, x_low, y, states, mixed_grad, row_coef, row_count
    )
    par_grad = jnp.sum(par_grad, axis=0)
    dt_grad, a_log_grad = heads_back(rv, u, e, dt_rows, log_decay, jnp.exp(a_full), row_count)
    dt_raw_grad = dt_grad * jax.nn.sigmoid(dt_pre)
    bc_sig = jax.nn.sigmoid(bc_pre)
    bc_grad = jnp.concatenate([b_grad, c_grad], axis=1) * (bc_sig * (1.0 + bc_pre * (1.0 - bc_sig)))
    bc_back, bc_taps, bc_bias = conv_small_back(bc_grad, bc_in, conv_w[DIN:].T, row_count)
    conv_w_grad = jnp.concatenate([par_grad[:KCONV], bc_taps], axis=1).T
    conv_b_grad = jnp.concatenate([par_grad[KCONV], bc_bias])
    skip_grad = jnp.sum(par_grad[5].reshape(HEADS, HEAD_DIM), axis=1)
    proj_grad = jnp.concatenate([z_grad, x_grad, low16(bc_back), low16(dt_raw_grad)], axis=1)
    normed_grad = lax.dot_general(
        proj_grad, gathered[0], (((1,), (1,)), ((), ())), preferred_element_type=jnp.float32
    )
    source_grad, normgain_grad = front_back(normed_grad)
    token_grad = (cot_rows + source_grad).astype(jnp.bfloat16)
    owned = settle_grads(
        normed_low,
        proj_grad,
        mixed_low,
        branch_grad,
        normgain_grad,
        conv_w_grad,
        conv_b_grad,
        par_grad[6],
        (a_log_grad, jnp.sum(dt_raw_grad, axis=0), skip_grad),
    )
    return (
        output,
        token_grad,
        owned[0],
        owned[1],
        owned[2],
        owned[3],
        owned[4],
        owned[5],
        owned[6],
        owned[7],
        owned[8],
    )


def solution(mesh):
    in_specs = (
        P(("wide", "narrow"), None),
        P(("wide", "narrow")),
        P(("wide", "narrow"), None),
        P(("wide", "narrow"), None),
        P(("wide", "narrow")),
        P(("wide", "narrow"), None),
        P(("wide", "narrow")),
        P(("wide", "narrow")),
        P("wide"),
        P("wide"),
        P("wide"),
        P(("wide", "narrow"), None),
    )
    out_specs = (
        P(("wide", "narrow"), None),
        P(("wide", "narrow"), None),
        P(("wide", "narrow"), None),
        P(("wide", "narrow"), None),
        P(("wide", "narrow")),
        P(("wide", "narrow"), None),
        P(("wide", "narrow")),
        P(("wide", "narrow")),
        P("wide"),
        P("wide"),
        P("wide"),
    )
    return jax.shard_map(body, mesh=mesh, in_specs=in_specs, out_specs=out_specs, check_vma=False)
```
